32 devices in a mesh: group: 2 (over x), src: 16 (over z, y, core).
Axes of the slice: x: 2, y: 2, z: 4, core: 2. Of those that a mesh axis runs over, the one named last changes fastest.
Arguments:
- positions: float32 [2, 32768], P(None, ('group', 'src')), parts along dimension 1, may hold values from -0.2 to 0.2
- flux: float32 [4, 32768], P(None, ('group', 'src')), parts along dimension 1, may hold values from 0.1 to 2
- cluster: int32 [32768], P(('group', 'src')), parts along dimension 0, may hold values from 0 to 15
- jones: float32 [4, 2, 16, 1024], P(None, None, None, ('group', 'src')), parts along dimension 3, may hold values from -4 to 4
- station_uvw: float32 [3, 1024], P(None, ('group', 'src')), parts along dimension 1, may hold values from -600 to 600
- channels: int32 [8], P('group'), parts along dimension 0, may hold values from 0 to 383
- tile_map: int32 [32, 2], P('group'), parts along dimension 0, may hold values from 0 to 15, as said below
Outputs:
- visibilities: float32 [32, 4, 2, 1024], P(('group', 'src')), parts along dimension 0
The draws below stay inside these ranges and needn't reach their ends.
There are 2 independent parts, one for each index of `group`. The reference program is written for one: setup_inputs(seed, part) draws one part's arguments, and reference() takes and returns one part's arrays. A program takes and returns all parts, laid end to end along the dimension named above; each array names one. Nothing has to cross between parts.
Inputs may be any that keep to these rules, and one draw needn't show every extreme that they name: `tile_map`: each row is a pair of station tiles (first, second) with first <= second; the 16 pairs are distinct.
All inputs are finite; a program needn't handle non-finite values.
Results may differ from the reference program's by a relative error of at most 0.0038.
Values sent between devices are 32-bit elements; how exact they have to be, the bound alone decides.
A program may use at most 128 MiB of HBM per device.

```python
import math
import jax
import jax.numpy as jnp
import numpy as np
from jax import lax

S = 512
C = 4
K = 16
TS = 32
SOURCES = 16384
BLOCKS = 16


def draw_tile_map(key, part):
    tiles = S // TS
    table = np.array([(first, second) for first in range(tiles) for second in range(first, tiles)], np.int32)
    count = table.shape[0]
    key_one, key_two = jax.random.split(jax.random.fold_in(key, 7))
    scores = jax.random.randint(key_one, (count,), 0, 1 << 20) * 256 + jnp.arange(count, dtype=jnp.int32)
    scores = scores.at[tiles - 1].set(1 << 29)
    order = jnp.argsort(-scores, stable=True)[:BLOCKS]
    shuffle = jax.random.permutation(key_two, BLOCKS)
    chosen = order[shuffle]
    return jnp.asarray(table)[chosen]


def place_ends(values, own_key, smallest, high):
    dims = values.shape
    index_at = [jax.random.randint(jax.random.fold_in(own_key, axis), (), 0, dims[axis]) for axis in range(len(dims))]
    values = values.at[tuple(index_at)].set(smallest)
    longest = dims.index(max(dims))
    index_at[longest] = (index_at[longest] + 1) % dims[longest]
    return values.at[tuple(index_at)].set(high)


def block_levels(own_key, dims, cuts, smallest, high):
    factor_of, own = 1.0, jax.random.fold_in(own_key, 6)
    for dim, parts in cuts:
        steps = jnp.exp(jax.random.uniform(jax.random.fold_in(own, dim), (parts,), jnp.float32, smallest / len(cuts), high / len(cuts)))
        factor_of = factor_of * jnp.repeat(steps, dims[dim] // parts).reshape([-1 if axis == dim else 1 for axis in range(len(dims))])
    return factor_of


def gaussian(rng, extent, spread, limit, cuts=(), held_as=jnp.bfloat16):
    gain = block_levels(rng, extent, cuts, -0.22, 0.18) if cuts else 1.0
    drawn = jax.random.normal(rng, extent, jnp.float32) * spread * gain
    return jnp.minimum(jnp.maximum(drawn, -limit), limit).astype(held_as)


def setup_inputs(seed: int = 0, part: int = 0) -> dict:
    splits = jax.random.split(jax.random.key(seed), 8)
    part_splits = jax.random.split(jax.random.fold_in(splits[7], part), 8)
    return {
        "positions": jnp.clip(jax.random.uniform(part_splits[0], (2, SOURCES), jnp.float32, -0.2, 0.2) * block_levels(part_splits[0], (2, SOURCES), ((1, 16),), -0.4, 0.0), -0.2, 0.2),
        "flux": jnp.clip(jnp.exp(math.log(2.0) - 2.9957323 * jax.random.uniform(part_splits[1], (C, SOURCES), jnp.float32) ** block_levels(part_splits[1], (C, SOURCES), ((1, 16),), -0.2, 0.2)), 0.1, 2.0),
        "cluster": place_ends(jax.random.randint(part_splits[2], (SOURCES,), 0, K), jax.random.fold_in(part_splits[2], 1), 0, K - 1).astype(jnp.int32),
        "jones": gaussian(part_splits[3], (C, 2, K, S), 0.7, 4.0, ((3, 16),), jnp.float32),
        "station_uvw": gaussian(part_splits[4], (3, S), 100.0, 600.0, ((1, 16),), jnp.float32),
        "channels": place_ends(jax.random.randint(part_splits[5], (C,), 0, 384), jax.random.fold_in(part_splits[5], 1), 0, 383).astype(jnp.int32),
        "tile_map": draw_tile_map(jax.random.fold_in(jax.random.fold_in(splits[7], part), 71), part),
    }


def phasors(station_gain, coords_uvw, coords, cluster_val, freq_ratio):
    directions = station_gain.shape[2]
    onehot = (cluster_val[None, :] == jnp.arange(directions, dtype=jnp.float32)[:, None]).astype(jnp.float32)
    gain_re = jnp.einsum('ckp,kn->cpn', station_gain[:, 0], onehot, precision=lax.Precision.HIGHEST)
    gain_im = jnp.einsum('ckp,kn->cpn', station_gain[:, 1], onehot, precision=lax.Precision.HIGHEST)
    l_term = coords[0]
    m_term = coords[1]
    n_term = jnp.sqrt(1.0 - l_term * l_term - m_term * m_term)
    argument = coords_uvw[0][:, None] * l_term[None, :] + coords_uvw[1][:, None] * m_term[None, :] + coords_uvw[2][:, None] * (n_term - 1.0)[None, :]
    phase = (2.0 * math.pi * freq_ratio)[:, None, None] * argument[None]
    cosine = jnp.cos(phase)
    sine = jnp.sin(phase)
    real_part = gain_re * cosine + gain_im * sine
    imag_part = gain_im * cosine - gain_re * sine
    return (real_part, imag_part)

def weighted_side(real_part, imag_part, fluxes, scale):
    weight = fluxes[:, None, :] * scale
    return jnp.stack([real_part * weight, imag_part * weight], 2).astype(jnp.bfloat16)

def plain_side(real_part, imag_part):
    return jnp.stack([real_part, imag_part], 2).astype(jnp.bfloat16)

def reference(positions, flux, cluster, jones, station_uvw, channels, tile_map):
    freq_ratio = 1.0 + 0.002 * channels.astype(jnp.float32)
    scale = 1.0 / math.sqrt(SOURCES)
    width = math.gcd(SOURCES, 4096)
    turns = SOURCES // width
    first_tile = tile_map[:, 0]
    second_tile = tile_map[:, 1]
    tiles = S // TS
    chans = jones.shape[0]

    def accumulate(total, turn):
        begin = (turn * width).astype(jnp.int32)
        coords = lax.dynamic_slice_in_dim(positions, begin, width, 1)
        fluxes = lax.dynamic_slice_in_dim(flux, begin, width, 1)
        cluster_val = lax.dynamic_slice_in_dim(cluster, begin, width, 0).astype(jnp.float32)
        real_part, imag_part = phasors(jones, station_uvw, coords, cluster_val, freq_ratio)
        weighted = weighted_side(real_part, imag_part, fluxes, scale).reshape(chans, tiles, TS, 2, width)
        plain = plain_side(real_part, imag_part).reshape(chans, tiles, TS, 2, width)
        left_sel = jnp.take(weighted, first_tile, axis=1).astype(jnp.float32)
        right_sel = jnp.take(plain, second_tile, axis=1).astype(jnp.float32)
        real_sum = jnp.einsum('cbirx,cbjrx->bcij', left_sel, right_sel)
        imag_sum = jnp.einsum('cbix,cbjx->bcij', left_sel[:, :, :, 1], right_sel[:, :, :, 0]) - jnp.einsum('cbix,cbjx->bcij', left_sel[:, :, :, 0], right_sel[:, :, :, 1])
        return (total + jnp.stack([real_sum, imag_sum], 2), None)
    blocks = tile_map.shape[0]
    start_total = jnp.zeros((blocks, chans, 2, TS, TS), jnp.float32)
    total, unused = lax.scan(accumulate, start_total, jnp.arange(turns, dtype=jnp.int32))
    same_tile = (first_tile == second_tile)[:, None, None, None, None]
    diagonal = (jnp.arange(TS)[:, None] == jnp.arange(TS)[None, :])[None, None, None]
    total = jnp.where(same_tile & diagonal, jnp.float32(0.0), total)
    return total.reshape(blocks, chans, 2, TS * TS)
```

```python
import functools
import math

import jax
import jax.numpy as jnp
from jax import lax
from jax.experimental import pallas as pl
from jax.experimental.pallas import tpu as pltpu
from jax.sharding import PartitionSpec as P

MESH = pl.DeviceIdType.MESH
TS = 32
GROUP = 64
HALF = 32
CHUNK = 256
MAGIC = 12582912.0
COS = (
    0.9999992251396179,
    -19.738977432250977,
    64.9285888671875,
    -85.27084350585938,
    58.78694152832031,
    -21.0654296875,
)
SIN = (
    6.283185005187988,
    -41.34158706665039,
    81.59991455078125,
    -76.61414337158203,
    41.341365814208984,
    -12.468818664550781,
)


def horner(coefs, y):
    total = jnp.float32(coefs[-1])
    for coef in coefs[-2::-1]:
        total = total * y + jnp.float32(coef)
    return total


def three_parts(value):
    first = value.astype(jnp.bfloat16).astype(jnp.float32)
    rest = value - first
    second = rest.astype(jnp.bfloat16).astype(jnp.float32)
    return first, second, rest - second


def kernel(
    devices,
    chans,
    dirs,
    scale,
    tile_ref,
    station_ref,
    source_ref,
    out_ref,
    stations,
    sources,
    table,
    onehots,
    acc,
    st_send,
    st_recv,
    st_fwd_send,
    st_fwd_recv,
    so_send,
    so_recv,
    so_fwd_send,
    so_fwd_recv,
    own_sem,
):
    chips = devices // 2
    me = lax.axis_index("src")
    chip = me // 2
    core = lax.rem(me, 2)
    partner = chip * 2 + 1 - core
    rows = stations.shape[1]
    per_dev = rows * 2 // chans
    width = sources.shape[2]

    own = [
        pltpu.make_async_copy(station_ref, stations.at[me], own_sem.at[0]),
        pltpu.make_async_copy(source_ref, sources.at[me], own_sem.at[1]),
    ]
    for copy in own:
        copy.start()

    barrier = pltpu.get_barrier_semaphore()

    def greet(k, carry):
        there = lax.rem(chip + k, chips) * 2 + core
        pl.semaphore_signal(barrier, inc=1, device_id={"src": there}, device_id_type=MESH)
        return carry

    pl.semaphore_signal(barrier, inc=1, device_id={"src": partner}, device_id_type=MESH)
    lax.fori_loop(1, chips, greet, 0)
    pl.semaphore_wait(barrier, chips)

    def direct(mine, slots, send, recv, k):
        there = lax.rem(chip + k, chips) * 2 + core
        return pltpu.make_async_remote_copy(
            src_ref=mine,
            dst_ref=slots.at[me],
            send_sem=send.at[k],
            recv_sem=recv.at[k],
            device_id={"src": there},
            device_id_type=MESH,
        )

    def arrival(mine, slots, send, recv, k):
        came = lax.rem(chip - k + chips, chips) * 2 + core
        return pltpu.make_async_remote_copy(
            src_ref=mine,
            dst_ref=slots.at[came],
            send_sem=send.at[k],
            recv_sem=recv.at[k],
            device_id={"src": partner},
            device_id_type=MESH,
        )

    def forward(slots, send, recv, k):
        came = lax.rem(chip - k + chips, chips) * 2 + core
        return pltpu.make_async_remote_copy(
            src_ref=slots.at[came],
            dst_ref=slots.at[came],
            send_sem=send.at[k],
            recv_sem=recv.at[k],
            device_id={"src": partner},
            device_id_type=MESH,
        )

    def forwarded(slots, send, recv, k):
        came = lax.rem(chip - k + chips, chips) * 2 + 1 - core
        return pltpu.make_async_remote_copy(
            src_ref=slots.at[came],
            dst_ref=slots.at[came],
            send_sem=send.at[k],
            recv_sem=recv.at[k],
            device_id={"src": partner},
            device_id_type=MESH,
        )

    for copy in own:
        copy.wait()
    forward(stations, st_fwd_send, st_fwd_recv, 0).start()

    def send_stations(k, carry):
        direct(station_ref, stations, st_send, st_recv, k).start()
        return carry

    lax.fori_loop(1, chips, send_stations, 0)
    forward(sources, so_fwd_send, so_fwd_recv, 0).start()

    def send_sources(k, carry):
        direct(source_ref, sources, so_send, so_recv, k).start()
        return carry

    lax.fori_loop(1, chips, send_sources, 0)

    onehots[3 * GROUP :, :] = jnp.zeros((GROUP, width), jnp.bfloat16)
    for part in range(3):
        onehots[part * GROUP + HALF + dirs : (part + 1) * GROUP, :] = jnp.zeros(
            (GROUP - HALF - dirs, width), jnp.bfloat16
        )
    acc[...] = jnp.zeros_like(acc)

    def relay_stations(k, carry):
        arrival(station_ref, stations, st_send, st_recv, k).wait_recv()
        forward(stations, st_fwd_send, st_fwd_recv, k).start()
        return carry

    lax.fori_loop(1, chips, relay_stations, 0)

    def take_stations(k, carry):
        forwarded(stations, st_fwd_send, st_fwd_recv, k).wait_recv()
        return carry

    lax.fori_loop(0, chips, take_stations, 0)

    per_tile = TS // per_dev
    lane = lax.broadcasted_iota(jnp.int32, (TS, 128), 1)
    is_phase = lax.rem(lane, GROUP) < HALF
    low = lane < GROUP
    half_rows = chans * TS
    tiles = [tile_ref[me, 0], tile_ref[me, 1]]
    for side in range(2):
        held = [stations[tiles[side] * per_tile + d] for d in range(per_tile)]
        for c in range(chans):
            begin = c // 2 * per_dev
            value = jnp.concatenate([part[begin : begin + per_dev] for part in held], 0)
            if c % 2:
                value = pltpu.roll(value, GROUP, 1)
            value = jnp.where(low, value, 0.0)
            first, second, third = three_parts(value)
            pieces = [first + pltpu.roll(second, GROUP, 1), third]
            at = side * half_rows + c * TS
            for index, piece in enumerate(pieces):
                cols = slice(index * 128, index * 128 + 128)
                table[at : at + TS, cols] = jnp.where(is_phase, piece, 0.0).astype(jnp.bfloat16)
                below = 2 * half_rows + at
                table[below : below + TS, cols] = jnp.where(is_phase, 0.0, piece).astype(
                    jnp.bfloat16
                )

    def block(step, carry):
        k = step // 2
        odd = lax.rem(step, 2)

        @pl.when(jnp.logical_and(odd == 0, k > 0))
        def _():
            arrival(source_ref, sources, so_send, so_recv, k).wait_recv()
            forward(sources, so_fwd_send, so_fwd_recv, k).start()

        @pl.when(odd == 1)
        def _():
            forwarded(sources, so_fwd_send, so_fwd_recv, k).wait_recv()

        flip = core + odd - 2 * core * odd
        came = lax.rem(chip - k + chips, chips) * 2 + flip
        l_term = sources[came, 0:1, :]
        m_term = sources[came, 1:2, :]
        kinds = sources[came, 2 + chans : 3 + chans, :]
        n_less = jnp.sqrt(1.0 - l_term * l_term - m_term * m_term) - 1.0
        sub = lax.broadcasted_iota(jnp.int32, (16, width), 0)
        coords = jnp.zeros((16, width), jnp.float32)
        for axis, term in enumerate((l_term, m_term, n_less)):
            for index, part in enumerate(three_parts(term)):
                coords = jnp.where(sub == index * 3 + axis, part, coords)
        kind_rows = lax.broadcasted_iota(jnp.int32, (dirs, width), 0).astype(jnp.float32)
        onehot = jnp.where(kind_rows == kinds, 1.0, 0.0).astype(jnp.bfloat16)
        coords = coords.astype(jnp.bfloat16)
        for part in range(3):
            base = part * GROUP
            onehots[base : base + dirs, :] = onehot
            onehots[base + dirs : base + dirs + 16, :] = coords
            onehots[base + HALF : base + HALF + dirs, :] = onehot

        total = acc[...]
        for chunk in range(width // CHUNK):
            cols = slice(chunk * CHUNK, chunk * CHUNK + CHUNK)
            weights = onehots[:, cols]
            sides = []
            for side in range(2):
                real, imag = [], []
                for c in range(chans):
                    at = side * half_rows + c * TS
                    below = 2 * half_rows + at
                    turns = jnp.dot(
                        table[at : at + TS, :], weights, preferred_element_type=jnp.float32
                    )
                    size = jnp.dot(
                        table[below : below + TS, :], weights, preferred_element_type=jnp.float32
                    )
                    if side == 0:
                        size = size * (sources[came, 2 + c : 3 + c, cols] * scale)
                    turns = turns - ((turns + MAGIC) - MAGIC)
                    square = turns * turns
                    real.append((size * horner(COS, square)).astype(jnp.bfloat16))
                    imag.append((size * (turns * horner(SIN, square))).astype(jnp.bfloat16))
                sides.append(jnp.concatenate(real + imag, 0))
            total = total + lax.dot_general(
                sides[0],
                sides[1],
                (((1,), (1,)), ((), ())),
                preferred_element_type=jnp.float32,
            )
        acc[...] = total
        return carry

    lax.fori_loop(0, 2 * chips, block, 0)

    same = tiles[0] == tiles[1]
    diagonal = lax.broadcasted_iota(jnp.int32, (TS, TS), 0) == lax.broadcasted_iota(
        jnp.int32, (TS, TS), 1
    )
    clear = jnp.logical_and(diagonal, same)
    for c in range(chans):
        top = slice(c * TS, c * TS + TS)
        low_rows = slice(half_rows + c * TS, half_rows + c * TS + TS)
        real_rows = acc[top, :]
        imag_rows = acc[low_rows, :]
        real = real_rows[:, top] + imag_rows[:, low_rows]
        imag = real_rows[:, low_rows] - imag_rows[:, top]
        for part, value in enumerate((real, imag)):
            value = jnp.where(clear, 0.0, value)
            for i in range(TS):
                out_ref[0, c, part : part + 1, i * TS : i * TS + TS] = value[i : i + 1, :]

    def finish(k, carry):
        direct(station_ref, stations, st_send, st_recv, k).wait_send()
        direct(source_ref, sources, so_send, so_recv, k).wait_send()
        return carry

    lax.fori_loop(1, chips, finish, 0)

    def finish_forward(k, carry):
        forward(stations, st_fwd_send, st_fwd_recv, k).wait_send()
        forward(sources, so_fwd_send, so_fwd_recv, k).wait_send()
        return carry

    lax.fori_loop(0, chips, finish_forward, 0)


def on_device(positions, flux, cluster, jones, station_uvw, channels, tile_map):
    freq_ratio = 1.0 + 0.002 * channels.astype(jnp.float32)
    width = positions.shape[1]
    devices = lax.axis_size("src")
    scale = 1.0 / math.sqrt(width * devices)
    chans, _, dirs, per_dev = jones.shape

    large = jnp.maximum(jnp.abs(jones[:, 0]), jnp.abs(jones[:, 1]))
    small = jnp.minimum(jnp.abs(jones[:, 0]), jnp.abs(jones[:, 1]))
    ratio = small / jnp.where(large > 0.0, large, 1.0)
    size = large * jnp.sqrt(1.0 + ratio * ratio)
    angle = jnp.arctan2(jones[:, 1], jones[:, 0]) * (-0.5 / math.pi)
    coords = freq_ratio[:, None, None] * station_uvw[None]
    features = jnp.concatenate(
        [
            angle,
            coords,
            coords,
            coords,
            jnp.zeros((chans, HALF - dirs - 9, per_dev), jnp.float32),
            size,
            jnp.zeros((chans, GROUP - HALF - dirs, per_dev), jnp.float32),
        ],
        1,
    )
    own_stations = (
        features.reshape(chans // 2, 2 * GROUP, per_dev)
        .transpose(0, 2, 1)
        .reshape(chans // 2 * per_dev, 2 * GROUP)
    )
    own_sources = jnp.concatenate(
        [
            positions,
            flux,
            cluster.astype(jnp.float32)[None],
            jnp.zeros((8 - 3 - chans, width), jnp.float32),
        ],
        0,
    )
    wide = 2 * chans * TS
    chips = devices // 2
    vmem = pl.BlockSpec(memory_space=pltpu.VMEM)
    return pl.pallas_call(
        functools.partial(kernel, devices, chans, dirs, scale),
        out_shape=jax.ShapeDtypeStruct((1, chans, 2, TS * TS), jnp.float32),
        in_specs=[pl.BlockSpec(memory_space=pltpu.SMEM), vmem, vmem],
        out_specs=vmem,
        scratch_shapes=[
            pltpu.VMEM((devices,) + own_stations.shape, jnp.float32),
            pltpu.VMEM((devices,) + own_sources.shape, jnp.float32),
            pltpu.VMEM((2 * wide, 4 * GROUP), jnp.bfloat16),
            pltpu.VMEM((4 * GROUP, width), jnp.bfloat16),
            pltpu.VMEM((wide, wide), jnp.float32),
        ]
        + [pltpu.SemaphoreType.DMA((chips,))] * 8
        + [pltpu.SemaphoreType.DMA((2,))],
        compiler_params=pltpu.CompilerParams(collective_id=0, has_side_effects=True),
    )(tile_map, own_stations, own_sources)


def solution(mesh):
    in_specs = (
        P(None, ("group", "src")),
        P(None, ("group", "src")),
        P(("group", "src")),
        P(None, None, None, ("group", "src")),
        P(None, ("group", "src")),
        P("group"),
        P("group", None),
    )
    out_specs = P(("group", "src"), None, None, None)
    return jax.shard_map(
        on_device, mesh=mesh, in_specs=in_specs, out_specs=out_specs, check_vma=False
    )
```

```python
import functools
import math

import jax
import jax.numpy as jnp
from jax import lax
from jax.experimental import pallas as pl
from jax.experimental.pallas import tpu as pltpu
from jax.sharding import PartitionSpec as P

MESH = pl.DeviceIdType.MESH
TS = 32
GROUP = 64
HALF = 32
CHUNK = 256
SINE = (3.1415820121765137, -5.167142868041992, 2.5418992042541504, -0.5546366572380066)
ONE = 1.0 + 6e-7


def horner(coefs, y):
    total = jnp.float32(coefs[-1])
    for coef in coefs[-2::-1]:
        total = total * y + jnp.float32(coef)
    return total


def three_parts(value):
    first = value.astype(jnp.bfloat16).astype(jnp.float32)
    rest = value - first
    second = rest.astype(jnp.bfloat16).astype(jnp.float32)
    return first, second, rest - second


def kernel(
    devices,
    chans,
    dirs,
    scale,
    tile_ref,
    station_ref,
    source_ref,
    out_ref,
    stations,
    sources,
    table,
    onehots,
    sides,
    acc,
    st_send,
    st_recv,
    st_fwd_send,
    st_fwd_recv,
    so_send,
    so_recv,
    so_fwd_send,
    so_fwd_recv,
    own_sem,
):
    chips = devices // 2
    me = lax.axis_index("src")
    chip = me // 2
    core = lax.rem(me, 2)
    partner = chip * 2 + 1 - core
    rows = stations.shape[1]
    per_dev = rows * 2 // chans
    width = sources.shape[2]

    own = [
        pltpu.make_async_copy(station_ref, stations.at[me], own_sem.at[0]),
        pltpu.make_async_copy(source_ref, sources.at[me], own_sem.at[1]),
    ]
    for copy in own:
        copy.start()

    barrier = pltpu.get_barrier_semaphore()

    def greet(k, carry):
        there = lax.rem(chip + k, chips) * 2 + core
        pl.semaphore_signal(barrier, inc=1, device_id={"src": there}, device_id_type=MESH)
        return carry

    pl.semaphore_signal(barrier, inc=1, device_id={"src": partner}, device_id_type=MESH)
    lax.fori_loop(1, chips, greet, 0)
    pl.semaphore_wait(barrier, chips)

    def direct(mine, slots, send, recv, k):
        there = lax.rem(chip + k, chips) * 2 + core
        return pltpu.make_async_remote_copy(
            src_ref=mine,
            dst_ref=slots.at[me],
            send_sem=send.at[k],
            recv_sem=recv.at[k],
            device_id={"src": there},
            device_id_type=MESH,
        )

    def arrival(mine, slots, send, recv, k):
        came = lax.rem(chip - k + chips, chips) * 2 + core
        return pltpu.make_async_remote_copy(
            src_ref=mine,
            dst_ref=slots.at[came],
            send_sem=send.at[k],
            recv_sem=recv.at[k],
            device_id={"src": partner},
            device_id_type=MESH,
        )

    def forward(slots, send, recv, k):
        came = lax.rem(chip - k + chips, chips) * 2 + core
        return pltpu.make_async_remote_copy(
            src_ref=slots.at[came],
            dst_ref=slots.at[came],
            send_sem=send.at[k],
            recv_sem=recv.at[k],
            device_id={"src": partner},
            device_id_type=MESH,
        )

    def forwarded(slots, send, recv, k):
        came = lax.rem(chip - k + chips, chips) * 2 + 1 - core
        return pltpu.make_async_remote_copy(
            src_ref=slots.at[came],
            dst_ref=slots.at[came],
            send_sem=send.at[k],
            recv_sem=recv.at[k],
            device_id={"src": partner},
            device_id_type=MESH,
        )

    for copy in own:
        copy.wait()
    forward(stations, st_fwd_send, st_fwd_recv, 0).start()

    def send_stations(k, carry):
        direct(station_ref, stations, st_send, st_recv, k).start()
        return carry

    lax.fori_loop(1, chips, send_stations, 0)
    forward(sources, so_fwd_send, so_fwd_recv, 0).start()

    def send_sources(k, carry):
        direct(source_ref, sources, so_send, so_recv, k).start()
        return carry

    lax.fori_loop(1, chips, send_sources, 0)

    onehots[3 * GROUP :, :] = jnp.zeros((GROUP, width), jnp.bfloat16)
    for part in range(3):
        onehots[part * GROUP + HALF + dirs : (part + 1) * GROUP, :] = jnp.zeros(
            (GROUP - HALF - dirs, width), jnp.bfloat16
        )
    acc[...] = jnp.zeros_like(acc)

    def relay_stations(k, carry):
        arrival(station_ref, stations, st_send, st_recv, k).wait_recv()
        forward(stations, st_fwd_send, st_fwd_recv, k).start()
        return carry

    lax.fori_loop(1, chips, relay_stations, 0)

    def take_stations(k, carry):
        forwarded(stations, st_fwd_send, st_fwd_recv, k).wait_recv()
        return carry

    lax.fori_loop(0, chips, take_stations, 0)

    per_tile = TS // per_dev
    lane = lax.broadcasted_iota(jnp.int32, (TS, 128), 1)
    is_phase = lax.rem(lane, GROUP) < HALF
    low = lane < GROUP
    half_rows = chans * TS
    tiles = [tile_ref[me, 0], tile_ref[me, 1]]
    for side in range(2):
        held = [stations[tiles[side] * per_tile + d] for d in range(per_tile)]
        for c in range(chans):
            begin = c // 2 * per_dev
            value = jnp.concatenate([part[begin : begin + per_dev] for part in held], 0)
            if c % 2:
                value = pltpu.roll(value, GROUP, 1)
            value = jnp.where(low, value, 0.0)
            first, second, third = three_parts(value)
            pieces = [first + pltpu.roll(second, GROUP, 1), third]
            at = (side * chans + c) * 2 * TS
            for index, piece in enumerate(pieces):
                cols = slice(index * 128, index * 128 + 128)
                table[at : at + TS, cols] = jnp.where(is_phase, piece, 0.0).astype(jnp.bfloat16)
                below = at + TS
                table[below : below + TS, cols] = jnp.where(is_phase, 0.0, piece).astype(
                    jnp.bfloat16
                )

    def block(step, carry):
        k = step // 2
        odd = lax.rem(step, 2)

        @pl.when(jnp.logical_and(odd == 0, k > 0))
        def _():
            arrival(source_ref, sources, so_send, so_recv, k).wait_recv()
            forward(sources, so_fwd_send, so_fwd_recv, k).start()

        @pl.when(odd == 1)
        def _():
            forwarded(sources, so_fwd_send, so_fwd_recv, k).wait_recv()

        flip = core + odd - 2 * core * odd
        came = lax.rem(chip - k + chips, chips) * 2 + flip
        l_term = sources[came, 0:1, :]
        m_term = sources[came, 1:2, :]
        kinds = sources[came, 2 + chans : 3 + chans, :]
        n_less = jnp.sqrt(1.0 - l_term * l_term - m_term * m_term) - 1.0
        sub = lax.broadcasted_iota(jnp.int32, (16, width), 0)
        coords = jnp.zeros((16, width), jnp.float32)
        for axis, term in enumerate((l_term, m_term, n_less)):
            for index, part in enumerate(three_parts(term)):
                coords = jnp.where(sub == index * 3 + axis, part, coords)
        kind_rows = lax.broadcasted_iota(jnp.int32, (dirs, width), 0).astype(jnp.float32)
        onehot = jnp.where(kind_rows == kinds, 1.0, 0.0).astype(jnp.bfloat16)
        coords = coords.astype(jnp.bfloat16)
        for part in range(3):
            base = part * GROUP
            onehots[base : base + dirs, :] = onehot
            onehots[base + dirs : base + dirs + 16, :] = coords
            onehots[base + HALF : base + HALF + dirs, :] = onehot

        for chunk in range(width // CHUNK):
            cols = slice(chunk * CHUNK, chunk * CHUNK + CHUNK)
            weights = onehots[:, cols]
            found = jnp.dot(table[...], weights, preferred_element_type=jnp.float32)
            for side in range(2):
                for c in range(chans):
                    at = (side * chans + c) * 2 * TS
                    turns = found[at : at + TS]
                    double = found[at + TS : at + 2 * TS]
                    if side == 0:
                        double = double * (sources[came, 2 + c : 3 + c, cols] * scale)
                    turns = turns - jnp.round(turns)
                    sine = turns * horner(SINE, turns * turns)
                    square = sine * sine
                    rest = ONE - square
                    cosine = rest * lax.rsqrt(rest)
                    real = double * (0.5 - square)
                    imag = (double * sine) * cosine
                    top = c * TS
                    sides[side, top : top + TS, cols] = real.astype(jnp.bfloat16)
                    sides[side, half_rows + top : half_rows + top + TS, cols] = imag.astype(
                        jnp.bfloat16
                    )
        acc[...] += lax.dot_general(
            sides[0],
            sides[1],
            (((1,), (1,)), ((), ())),
            preferred_element_type=jnp.float32,
        )
        return carry

    lax.fori_loop(0, 2 * chips, block, 0)

    same = tiles[0] == tiles[1]
    diagonal = lax.broadcasted_iota(jnp.int32, (TS, TS), 0) == lax.broadcasted_iota(
        jnp.int32, (TS, TS), 1
    )
    clear = jnp.logical_and(diagonal, same)
    for c in range(chans):
        top = slice(c * TS, c * TS + TS)
        low_rows = slice(half_rows + c * TS, half_rows + c * TS + TS)
        real_rows = acc[top, :]
        imag_rows = acc[low_rows, :]
        real = real_rows[:, top] + imag_rows[:, low_rows]
        imag = real_rows[:, low_rows] - imag_rows[:, top]
        for part, value in enumerate((real, imag)):
            value = jnp.where(clear, 0.0, value)
            for i in range(TS):
                out_ref[0, c, part : part + 1, i * TS : i * TS + TS] = value[i : i + 1, :]

    def finish(k, carry):
        direct(station_ref, stations, st_send, st_recv, k).wait_send()
        direct(source_ref, sources, so_send, so_recv, k).wait_send()
        return carry

    lax.fori_loop(1, chips, finish, 0)

    def finish_forward(k, carry):
        forward(stations, st_fwd_send, st_fwd_recv, k).wait_send()
        forward(sources, so_fwd_send, so_fwd_recv, k).wait_send()
        return carry

    lax.fori_loop(0, chips, finish_forward, 0)


def on_device(positions, flux, cluster, jones, station_uvw, channels, tile_map):
    freq_ratio = 1.0 + 0.002 * channels.astype(jnp.float32)
    width = positions.shape[1]
    devices = lax.axis_size("src")
    scale = 1.0 / math.sqrt(width * devices)
    chans, _, dirs, per_dev = jones.shape

    large = jnp.maximum(jnp.abs(jones[:, 0]), jnp.abs(jones[:, 1]))
    small = jnp.minimum(jnp.abs(jones[:, 0]), jnp.abs(jones[:, 1]))
    ratio = small / jnp.where(large > 0.0, large, 1.0)
    size = large * jnp.sqrt(1.0 + ratio * ratio)
    angle = jnp.arctan2(jones[:, 1], jones[:, 0]) * (-0.5 / math.pi)
    coords = freq_ratio[:, None, None] * station_uvw[None]
    features = jnp.concatenate(
        [
            angle,
            coords,
            coords,
            coords,
            jnp.zeros((chans, HALF - dirs - 9, per_dev), jnp.float32),
            2.0 * size,
            jnp.zeros((chans, GROUP - HALF - dirs, per_dev), jnp.float32),
        ],
        1,
    )
    own_stations = (
        features.reshape(chans // 2, 2 * GROUP, per_dev)
        .transpose(0, 2, 1)
        .reshape(chans // 2 * per_dev, 2 * GROUP)
    )
    own_sources = jnp.concatenate(
        [
            positions,
            flux,
            cluster.astype(jnp.float32)[None],
            jnp.zeros((8 - 3 - chans, width), jnp.float32),
        ],
        0,
    )
    wide = 2 * chans * TS
    chips = devices // 2
    vmem = pl.BlockSpec(memory_space=pltpu.VMEM)
    return pl.pallas_call(
        functools.partial(kernel, devices, chans, dirs, scale),
        out_shape=jax.ShapeDtypeStruct((1, chans, 2, TS * TS), jnp.float32),
        in_specs=[pl.BlockSpec(memory_space=pltpu.SMEM), vmem, vmem],
        out_specs=vmem,
        scratch_shapes=[
            pltpu.VMEM((devices,) + own_stations.shape, jnp.float32),
            pltpu.VMEM((devices,) + own_sources.shape, jnp.float32),
            pltpu.VMEM((2 * wide, 4 * GROUP), jnp.bfloat16),
            pltpu.VMEM((4 * GROUP, width), jnp.bfloat16),
            pltpu.VMEM((2, wide, width), jnp.bfloat16),
            pltpu.VMEM((wide, wide), jnp.float32),
        ]
        + [pltpu.SemaphoreType.DMA((chips,))] * 8
        + [pltpu.SemaphoreType.DMA((2,))],
        compiler_params=pltpu.CompilerParams(collective_id=0, has_side_effects=True),
    )(tile_map, own_stations, own_sources)


def solution(mesh):
    in_specs = (
        P(None, ("group", "src")),
        P(None, ("group", "src")),
        P(("group", "src")),
        P(None, None, None, ("group", "src")),
        P(None, ("group", "src")),
        P("group"),
        P("group", None),
    )
    out_specs = P(("group", "src"), None, None, None)
    return jax.shard_map(
        on_device, mesh=mesh, in_specs=in_specs, out_specs=out_specs, check_vma=False
    )
```

```python
import functools
import math

import jax
import jax.numpy as jnp
from jax import lax
from jax.experimental import pallas as pl
from jax.experimental.pallas import tpu as pltpu
from jax.sharding import PartitionSpec as P

MESH = pl.DeviceIdType.MESH
TS = 32
GROUP = 64
HALF = 48
CHUNK = 256
SINE = (3.1415820121765137, -5.167142868041992, 2.5418992042541504, -0.5546366572380066)
ATAN = (
    0.15915492177009583,
    -0.05305047705769539,
    0.031808558851480484,
    -0.022538291290402412,
    0.016709571704268456,
    -0.011514591053128242,
    0.006331328768283129,
    -0.0022920165210962296,
    0.00039099203422665596,
)
ONE = 1.0 + 6e-7


def horner(coefs, y):
    total = jnp.float32(coefs[-1])
    for coef in coefs[-2::-1]:
        total = total * y + jnp.float32(coef)
    return total


def three_parts(value):
    first = value.astype(jnp.bfloat16).astype(jnp.float32)
    rest = value - first
    second = rest.astype(jnp.bfloat16).astype(jnp.float32)
    return first, second, rest - second


def polar(real, imag):
    wide, tall = jnp.abs(real), jnp.abs(imag)
    large, small = jnp.maximum(wide, tall), jnp.minimum(wide, tall)
    ratio = small / jnp.where(large > 0.0, large, 1.0)
    square = ratio * ratio
    size = large * jnp.sqrt(1.0 + square)
    angle = ratio * horner(ATAN, square)
    angle = jnp.where(tall > wide, 0.25 - angle, angle)
    angle = jnp.where(real < 0.0, 0.5 - angle, angle)
    return size, jnp.where(imag < 0.0, -angle, angle)


def kernel(
    devices,
    chans,
    dirs,
    scale,
    tile_ref,
    channel_ref,
    position_ref,
    flux_ref,
    cluster_ref,
    jones_ref,
    uvw_ref,
    out_ref,
    stations,
    sources,
    table,
    onehots,
    sides,
    acc,
    st_send,
    st_recv,
    st_fwd_send,
    st_fwd_recv,
    so_send,
    so_recv,
    so_fwd_send,
    so_fwd_recv,
):
    chips = devices // 2
    me = lax.axis_index("src")
    chip = me // 2
    core = lax.rem(me, 2)
    partner = chip * 2 + 1 - core
    rows = stations.shape[1]
    per_dev = rows * 2 // chans
    width = sources.shape[2]

    barrier = pltpu.get_barrier_semaphore()

    def greet(k, carry):
        there = lax.rem(chip + k, chips) * 2 + core
        pl.semaphore_signal(barrier, inc=1, device_id={"src": there}, device_id_type=MESH)
        return carry

    pl.semaphore_signal(barrier, inc=1, device_id={"src": partner}, device_id_type=MESH)
    lax.fori_loop(1, chips, greet, 0)

    l_own, m_own = position_ref[0:1, :], position_ref[1:2, :]
    sources[me, 0:2, :] = position_ref[...]
    sources[me, 2 : 2 + chans, :] = flux_ref[...]
    sources[me, 2 + chans : 3 + chans, :] = cluster_ref[...].astype(jnp.float32)
    sources[me, 3 + chans : 4 + chans, :] = jnp.sqrt(1.0 - l_own * l_own - m_own * m_own) - 1.0
    eight = lax.broadcasted_iota(jnp.int32, (8, per_dev), 0)
    coords = jnp.where(eight == 0, uvw_ref[0:1, :], 0.0)
    coords = jnp.where(eight == 1, uvw_ref[1:2, :], coords)
    coords = jnp.where(eight == 3 + chans, uvw_ref[2:3, :], coords)
    for pair in range(chans // 2):
        features = []
        for c in (2 * pair, 2 * pair + 1):
            freq_ratio = 1.0 + 0.002 * channel_ref[c].astype(jnp.float32)
            size, angle = polar(jones_ref[c, 0], jones_ref[c, 1])
            shifted = coords * freq_ratio
            features += [-angle, shifted, shifted, shifted]
            features += [jnp.zeros((HALF - dirs - 24, per_dev), jnp.float32), 2.0 * size]
        stations[me, pair * per_dev : (pair + 1) * per_dev, :] = jnp.concatenate(features, 0).T

    pl.semaphore_wait(barrier, chips)

    def direct(mine, slots, send, recv, k):
        there = lax.rem(chip + k, chips) * 2 + core
        return pltpu.make_async_remote_copy(
            src_ref=mine,
            dst_ref=slots.at[me],
            send_sem=send.at[k],
            recv_sem=recv.at[k],
            device_id={"src": there},
            device_id_type=MESH,
        )

    def arrival(mine, slots, send, recv, k):
        came = lax.rem(chip - k + chips, chips) * 2 + core
        return pltpu.make_async_remote_copy(
            src_ref=mine,
            dst_ref=slots.at[came],
            send_sem=send.at[k],
            recv_sem=recv.at[k],
            device_id={"src": partner},
            device_id_type=MESH,
        )

    def forward(slots, send, recv, k):
        came = lax.rem(chip - k + chips, chips) * 2 + core
        return pltpu.make_async_remote_copy(
            src_ref=slots.at[came],
            dst_ref=slots.at[came],
            send_sem=send.at[k],
            recv_sem=recv.at[k],
            device_id={"src": partner},
            device_id_type=MESH,
        )

    def forwarded(slots, send, recv, k):
        came = lax.rem(chip - k + chips, chips) * 2 + 1 - core
        return pltpu.make_async_remote_copy(
            src_ref=slots.at[came],
            dst_ref=slots.at[came],
            send_sem=send.at[k],
            recv_sem=recv.at[k],
            device_id={"src": partner},
            device_id_type=MESH,
        )

    forward(stations, st_fwd_send, st_fwd_recv, 0).start()

    def send_stations(k, carry):
        direct(stations.at[me], stations, st_send, st_recv, k).start()
        return carry

    lax.fori_loop(1, chips, send_stations, 0)
    onehots[3 * GROUP :, :] = jnp.zeros((GROUP, width), jnp.bfloat16)
    acc[...] = jnp.zeros_like(acc)

    def relay_stations(k, carry):
        arrival(stations.at[me], stations, st_send, st_recv, k).wait_recv()
        forward(stations, st_fwd_send, st_fwd_recv, k).start()
        return carry

    lax.fori_loop(1, chips, relay_stations, 0)

    forward(sources, so_fwd_send, so_fwd_recv, 0).start()

    def send_sources(k, carry):
        direct(sources.at[me], sources, so_send, so_recv, k).start()
        return carry

    lax.fori_loop(1, chips, send_sources, 0)

    def take_stations(k, carry):
        forwarded(stations, st_fwd_send, st_fwd_recv, k).wait_recv()
        return carry

    lax.fori_loop(0, chips, take_stations, 0)

    per_tile = TS // per_dev
    lane = lax.broadcasted_iota(jnp.int32, (TS, 128), 1)
    is_phase = lax.rem(lane, GROUP) < HALF
    low = lane < GROUP
    half_rows = chans * TS
    tiles = [tile_ref[me, 0], tile_ref[me, 1]]
    for side in range(2):
        held = [stations[tiles[side] * per_tile + d] for d in range(per_tile)]
        for c in range(chans):
            begin = c // 2 * per_dev
            value = jnp.concatenate([part[begin : begin + per_dev] for part in held], 0)
            if c % 2:
                value = pltpu.roll(value, GROUP, 1)
            value = jnp.where(low, value, 0.0)
            first, second, third = three_parts(value)
            pieces = [first + pltpu.roll(second, GROUP, 1), third]
            at = (side * chans + c) * 2 * TS
            for index, piece in enumerate(pieces):
                cols = slice(index * 128, index * 128 + 128)
                table[at : at + TS, cols] = jnp.where(is_phase, piece, 0.0).astype(jnp.bfloat16)
                below = at + TS
                table[below : below + TS, cols] = jnp.where(is_phase, 0.0, piece).astype(
                    jnp.bfloat16
                )

    def block(step, carry):
        k = step // 2
        odd = lax.rem(step, 2)

        @pl.when(jnp.logical_and(odd == 0, k > 0))
        def _():
            arrival(sources.at[me], sources, so_send, so_recv, k).wait_recv()
            forward(sources, so_fwd_send, so_fwd_recv, k).start()

        @pl.when(odd == 1)
        def _():
            forwarded(sources, so_fwd_send, so_fwd_recv, k).wait_recv()

        flip = core + odd - 2 * core * odd
        came = lax.rem(chip - k + chips, chips) * 2 + flip
        rows_in = sources[came]
        kinds = rows_in[2 + chans : 3 + chans, :]
        parts = three_parts(rows_in) + (jnp.zeros_like(rows_in),)
        kind_rows = lax.broadcasted_iota(jnp.int32, (dirs, width), 0).astype(jnp.float32)
        onehot = jnp.where(kind_rows == kinds, 1.0, 0.0).astype(jnp.bfloat16)
        upper = jnp.concatenate(parts[:2], 0).astype(jnp.bfloat16)
        lower = jnp.concatenate(parts[2:], 0).astype(jnp.bfloat16)
        for part in range(3):
            base = part * GROUP
            for index, value in enumerate((onehot, upper, lower, onehot)):
                onehots[base + index * 16 : base + index * 16 + 16, :] = value

        for chunk in range(width // CHUNK):
            cols = slice(chunk * CHUNK, chunk * CHUNK + CHUNK)
            weights = onehots[:, cols]
            found = jnp.dot(table[...], weights, preferred_element_type=jnp.float32)
            for side in range(2):
                for c in range(chans):
                    at = (side * chans + c) * 2 * TS
                    turns = found[at : at + TS]
                    double = found[at + TS : at + 2 * TS]
                    if side == 0:
                        double = double * (sources[came, 2 + c : 3 + c, cols] * scale)
                    turns = turns - jnp.round(turns)
                    sine = turns * horner(SINE, turns * turns)
                    square = sine * sine
                    rest = ONE - square
                    cosine = rest * lax.rsqrt(rest)
                    real = double * (0.5 - square)
                    imag = (double * sine) * cosine
                    top = c * TS
                    sides[side, top : top + TS, cols] = real.astype(jnp.bfloat16)
                    sides[side, half_rows + top : half_rows + top + TS, cols] = imag.astype(
                        jnp.bfloat16
                    )
        acc[...] += lax.dot_general(
            sides[0],
            sides[1],
            (((1,), (1,)), ((), ())),
            preferred_element_type=jnp.float32,
        )
        return carry

    lax.fori_loop(0, 2 * chips, block, 0)

    same = tiles[0] == tiles[1]
    diagonal = lax.broadcasted_iota(jnp.int32, (TS, TS), 0) == lax.broadcasted_iota(
        jnp.int32, (TS, TS), 1
    )
    clear = jnp.logical_and(diagonal, same)
    for c in range(chans):
        top = slice(c * TS, c * TS + TS)
        low_rows = slice(half_rows + c * TS, half_rows + c * TS + TS)
        real_rows = acc[top, :]
        imag_rows = acc[low_rows, :]
        real = real_rows[:, top] + imag_rows[:, low_rows]
        imag = real_rows[:, low_rows] - imag_rows[:, top]
        for part, value in enumerate((real, imag)):
            value = jnp.where(clear, 0.0, value)
            for i in range(TS):
                out_ref[0, c, part : part + 1, i * TS : i * TS + TS] = value[i : i + 1, :]

    def finish(k, carry):
        direct(stations.at[me], stations, st_send, st_recv, k).wait_send()
        direct(sources.at[me], sources, so_send, so_recv, k).wait_send()
        return carry

    lax.fori_loop(1, chips, finish, 0)

    def finish_forward(k, carry):
        forward(stations, st_fwd_send, st_fwd_recv, k).wait_send()
        forward(sources, so_fwd_send, so_fwd_recv, k).wait_send()
        return carry

    lax.fori_loop(0, chips, finish_forward, 0)


def on_device(positions, flux, cluster, jones, station_uvw, channels, tile_map):
    width = positions.shape[1]
    devices = lax.axis_size("src")
    scale = 1.0 / math.sqrt(width * devices)
    chans, _, dirs, per_dev = jones.shape

    wide = 2 * chans * TS
    chips = devices // 2
    vmem = pl.BlockSpec(memory_space=pltpu.VMEM)
    return pl.pallas_call(
        functools.partial(kernel, devices, chans, dirs, scale),
        out_shape=jax.ShapeDtypeStruct((1, chans, 2, TS * TS), jnp.float32),
        in_specs=[pl.BlockSpec(memory_space=pltpu.SMEM)] * 2 + [vmem] * 5,
        out_specs=vmem,
        scratch_shapes=[
            pltpu.VMEM((devices, chans // 2 * per_dev, 2 * GROUP), jnp.float32),
            pltpu.VMEM((devices, 8, width), jnp.float32),
            pltpu.VMEM((2 * wide, 4 * GROUP), jnp.bfloat16),
            pltpu.VMEM((4 * GROUP, width), jnp.bfloat16),
            pltpu.VMEM((2, wide, width), jnp.bfloat16),
            pltpu.VMEM((wide, wide), jnp.float32),
        ]
        + [pltpu.SemaphoreType.DMA((chips,))] * 8,
        compiler_params=pltpu.CompilerParams(collective_id=0, has_side_effects=True),
    )(tile_map, channels, positions, flux, cluster[None], jones, station_uvw)


def solution(mesh):
    in_specs = (
        P(None, ("group", "src")),
        P(None, ("group", "src")),
        P(("group", "src")),
        P(None, None, None, ("group", "src")),
        P(None, ("group", "src")),
        P("group"),
        P("group", None),
    )
    out_specs = P(("group", "src"), None, None, None)
    return jax.shard_map(
        on_device, mesh=mesh, in_specs=in_specs, out_specs=out_specs, check_vma=False
    )
```

```python
import functools
import math

import jax
import jax.numpy as jnp
from jax import lax
from jax.experimental import pallas as pl
from jax.experimental.pallas import tpu as pltpu
from jax.sharding import PartitionSpec as P

MESH = pl.DeviceIdType.MESH
TS = 32
GROUP = 64
HALF = 48
CHUNK = 256
SINE = (3.1415820121765137, -5.167142868041992, 2.5418992042541504, -0.5546366572380066)
ATAN = (
    0.15915492177009583,
    -0.05305047705769539,
    0.031808558851480484,
    -0.022538291290402412,
    0.016709571704268456,
    -0.011514591053128242,
    0.006331328768283129,
    -0.0022920165210962296,
    0.00039099203422665596,
)
ONE = 1.0 + 6e-7


def horner(coefs, y):
    total = jnp.float32(coefs[-1])
    for coef in coefs[-2::-1]:
        total = total * y + jnp.float32(coef)
    return total


def three_parts(value):
    first = value.astype(jnp.bfloat16).astype(jnp.float32)
    rest = value - first
    second = rest.astype(jnp.bfloat16).astype(jnp.float32)
    return first, second, rest - second


def polar(real, imag):
    wide, tall = jnp.abs(real), jnp.abs(imag)
    large, small = jnp.maximum(wide, tall), jnp.minimum(wide, tall)
    ratio = small / jnp.where(large > 0.0, large, 1.0)
    square = ratio * ratio
    size = large * jnp.sqrt(1.0 + square)
    angle = ratio * horner(ATAN, square)
    angle = jnp.where(tall > wide, 0.25 - angle, angle)
    angle = jnp.where(real < 0.0, 0.5 - angle, angle)
    return size, jnp.where(imag < 0.0, -angle, angle)


def kernel(
    devices,
    chans,
    dirs,
    scale,
    tile_ref,
    channel_ref,
    position_ref,
    flux_ref,
    cluster_ref,
    jones_ref,
    uvw_ref,
    out_ref,
    stations,
    sources,
    table,
    onehots,
    sides,
    acc,
    st_send,
    st_recv,
    st_fwd_send,
    st_fwd_recv,
    so_send,
    so_recv,
    so_fwd_send,
    so_fwd_recv,
):
    chips = devices // 2
    me = lax.axis_index("src")
    chip = me // 2
    core = lax.rem(me, 2)
    partner = chip * 2 + 1 - core
    rows = stations.shape[1]
    per_dev = rows * 2 // chans
    width = sources.shape[2]

    barrier = pltpu.get_barrier_semaphore()

    def greet(k, carry):
        there = lax.rem(chip + k, chips) * 2 + core
        pl.semaphore_signal(barrier, inc=1, device_id={"src": there}, device_id_type=MESH)
        return carry

    pl.semaphore_signal(barrier, inc=1, device_id={"src": partner}, device_id_type=MESH)
    lax.fori_loop(1, chips, greet, 0)

    l_own, m_own = position_ref[0:1, :], position_ref[1:2, :]
    sources[me, 0:2, :] = position_ref[...]
    sources[me, 2 : 2 + chans, :] = flux_ref[...]
    sources[me, 2 + chans : 3 + chans, :] = cluster_ref[...].astype(jnp.float32)
    sources[me, 3 + chans : 4 + chans, :] = jnp.sqrt(1.0 - l_own * l_own - m_own * m_own) - 1.0
    eight = lax.broadcasted_iota(jnp.int32, (8, per_dev), 0)
    coords = jnp.where(eight == 0, uvw_ref[0:1, :], 0.0)
    coords = jnp.where(eight == 1, uvw_ref[1:2, :], coords)
    coords = jnp.where(eight == 3 + chans, uvw_ref[2:3, :], coords)
    for pair in range(chans // 2):
        features = []
        for c in (2 * pair, 2 * pair + 1):
            freq_ratio = 1.0 + 0.002 * channel_ref[c].astype(jnp.float32)
            size, angle = polar(jones_ref[c, 0], jones_ref[c, 1])
            shifted = coords * freq_ratio
            features += [-angle, shifted, shifted, shifted]
            features += [jnp.zeros((HALF - dirs - 24, per_dev), jnp.float32), 2.0 * size]
        stations[me, pair * per_dev : (pair + 1) * per_dev, :] = jnp.concatenate(features, 0).T

    pl.semaphore_wait(barrier, chips)

    def direct(mine, slots, send, recv, k):
        there = lax.rem(chip + k, chips) * 2 + core
        return pltpu.make_async_remote_copy(
            src_ref=mine,
            dst_ref=slots.at[me],
            send_sem=send.at[k],
            recv_sem=recv.at[k],
            device_id={"src": there},
            device_id_type=MESH,
        )

    def arrival(mine, slots, send, recv, k):
        came = lax.rem(chip - k + chips, chips) * 2 + core
        return pltpu.make_async_remote_copy(
            src_ref=mine,
            dst_ref=slots.at[came],
            send_sem=send.at[k],
            recv_sem=recv.at[k],
            device_id={"src": partner},
            device_id_type=MESH,
        )

    def forward(slots, send, recv, k):
        came = lax.rem(chip - k + chips, chips) * 2 + core
        return pltpu.make_async_remote_copy(
            src_ref=slots.at[came],
            dst_ref=slots.at[came],
            send_sem=send.at[k],
            recv_sem=recv.at[k],
            device_id={"src": partner},
            device_id_type=MESH,
        )

    def forwarded(slots, send, recv, k):
        came = lax.rem(chip - k + chips, chips) * 2 + 1 - core
        return pltpu.make_async_remote_copy(
            src_ref=slots.at[came],
            dst_ref=slots.at[came],
            send_sem=send.at[k],
            recv_sem=recv.at[k],
            device_id={"src": partner},
            device_id_type=MESH,
        )

    forward(stations, st_fwd_send, st_fwd_recv, 0).start()

    def send_stations(k, carry):
        direct(stations.at[me], stations, st_send, st_recv, k).start()
        return carry

    lax.fori_loop(1, chips, send_stations, 0)
    onehots[:, 3 * GROUP :, :] = jnp.zeros((2, GROUP, width), jnp.bfloat16)
    sides[1] = jnp.zeros(sides.shape[1:], jnp.bfloat16)
    acc[...] = jnp.zeros_like(acc)

    def relay_stations(k, carry):
        arrival(stations.at[me], stations, st_send, st_recv, k).wait_recv()
        forward(stations, st_fwd_send, st_fwd_recv, k).start()
        return carry

    lax.fori_loop(1, chips, relay_stations, 0)

    forward(sources, so_fwd_send, so_fwd_recv, 0).start()

    def send_sources(k, carry):
        direct(sources.at[me], sources, so_send, so_recv, k).start()
        return carry

    lax.fori_loop(1, chips, send_sources, 0)

    def take_stations(k, carry):
        forwarded(stations, st_fwd_send, st_fwd_recv, k).wait_recv()
        return carry

    lax.fori_loop(0, chips, take_stations, 0)

    per_tile = TS // per_dev
    lane = lax.broadcasted_iota(jnp.int32, (TS, 128), 1)
    is_phase = lax.rem(lane, GROUP) < HALF
    low = lane < GROUP
    half_rows = chans * TS
    tiles = [tile_ref[me, 0], tile_ref[me, 1]]
    for side in range(2):
        held = [stations[tiles[side] * per_tile + d] for d in range(per_tile)]
        for c in range(chans):
            begin = c // 2 * per_dev
            value = jnp.concatenate([part[begin : begin + per_dev] for part in held], 0)
            if c % 2:
                value = pltpu.roll(value, GROUP, 1)
            value = jnp.where(low, value, 0.0)
            first, second, third = three_parts(value)
            pieces = [first + pltpu.roll(second, GROUP, 1), third]
            at = (side * chans + c) * 2 * TS
            for index, piece in enumerate(pieces):
                cols = slice(index * 128, index * 128 + 128)
                table[at : at + TS, cols] = jnp.where(is_phase, piece, 0.0).astype(jnp.bfloat16)
                below = at + TS
                table[below : below + TS, cols] = jnp.where(is_phase, 0.0, piece).astype(
                    jnp.bfloat16
                )

    contract = (((1,), (1,)), ((), ()))

    def predict(slot, came):
        rows_in = sources[came]
        kinds = rows_in[2 + chans : 3 + chans, :]
        parts = three_parts(rows_in) + (jnp.zeros_like(rows_in),)
        kind_rows = lax.broadcasted_iota(jnp.int32, (dirs, width), 0).astype(jnp.float32)
        onehot = jnp.where(kind_rows == kinds, 1.0, 0.0).astype(jnp.bfloat16)
        upper = jnp.concatenate(parts[:2], 0).astype(jnp.bfloat16)
        lower = jnp.concatenate(parts[2:], 0).astype(jnp.bfloat16)
        for part in range(3):
            base = part * GROUP
            for index, value in enumerate((onehot, upper, lower, onehot)):
                onehots[slot, base + index * 16 : base + index * 16 + 16, :] = value

        for chunk in range(width // CHUNK):
            cols = slice(chunk * CHUNK, chunk * CHUNK + CHUNK)
            weights = onehots[slot, :, cols]
            found = jnp.dot(table[...], weights, preferred_element_type=jnp.float32)
            for side in range(2):
                for c in range(chans):
                    at = (side * chans + c) * 2 * TS
                    turns = found[at : at + TS]
                    double = found[at + TS : at + 2 * TS]
                    if side == 0:
                        double = double * (sources[came, 2 + c : 3 + c, cols] * scale)
                    turns = turns - jnp.round(turns)
                    sine = turns * horner(SINE, turns * turns)
                    square = sine * sine
                    rest = ONE - square
                    cosine = rest * lax.rsqrt(rest)
                    real = double * (0.5 - square)
                    imag = (double * sine) * cosine
                    top = c * TS
                    sides[slot, side, top : top + TS, cols] = real.astype(jnp.bfloat16)
                    sides[slot, side, half_rows + top : half_rows + top + TS, cols] = imag.astype(
                        jnp.bfloat16
                    )

    def add_products(slot):
        acc[...] += lax.dot_general(
            sides[slot, 0], sides[slot, 1], contract, preferred_element_type=jnp.float32
        )

    def step(k, carry):
        @pl.when(k > 0)
        def _():
            arrival(sources.at[me], sources, so_send, so_recv, k).wait_recv()
            forward(sources, so_fwd_send, so_fwd_recv, k).start()

        forwarded(sources, so_fwd_send, so_fwd_recv, k).wait_recv()
        came = lax.rem(chip - k + chips, chips) * 2
        predict(0, came + core)
        add_products(1)
        predict(1, came + 1 - core)
        add_products(0)
        return carry

    lax.fori_loop(0, chips, step, 0)
    add_products(1)

    same = tiles[0] == tiles[1]
    diagonal = lax.broadcasted_iota(jnp.int32, (TS, TS), 0) == lax.broadcasted_iota(
        jnp.int32, (TS, TS), 1
    )
    clear = jnp.logical_and(diagonal, same)
    for c in range(chans):
        top = slice(c * TS, c * TS + TS)
        low_rows = slice(half_rows + c * TS, half_rows + c * TS + TS)
        real_rows = acc[top, :]
        imag_rows = acc[low_rows, :]
        real = real_rows[:, top] + imag_rows[:, low_rows]
        imag = real_rows[:, low_rows] - imag_rows[:, top]
        for part, value in enumerate((real, imag)):
            value = jnp.where(clear, 0.0, value)
            for i in range(TS):
                out_ref[0, c, part : part + 1, i * TS : i * TS + TS] = value[i : i + 1, :]

    def finish(k, carry):
        direct(stations.at[me], stations, st_send, st_recv, k).wait_send()
        direct(sources.at[me], sources, so_send, so_recv, k).wait_send()
        return carry

    lax.fori_loop(1, chips, finish, 0)

    def finish_forward(k, carry):
        forward(stations, st_fwd_send, st_fwd_recv, k).wait_send()
        forward(sources, so_fwd_send, so_fwd_recv, k).wait_send()
        return carry

    lax.fori_loop(0, chips, finish_forward, 0)


def on_device(positions, flux, cluster, jones, station_uvw, channels, tile_map):
    width = positions.shape[1]
    devices = lax.axis_size("src")
    scale = 1.0 / math.sqrt(width * devices)
    chans, _, dirs, per_dev = jones.shape

    wide = 2 * chans * TS
    chips = devices // 2
    vmem = pl.BlockSpec(memory_space=pltpu.VMEM)
    return pl.pallas_call(
        functools.partial(kernel, devices, chans, dirs, scale),
        out_shape=jax.ShapeDtypeStruct((1, chans, 2, TS * TS), jnp.float32),
        in_specs=[pl.BlockSpec(memory_space=pltpu.SMEM)] * 2 + [vmem] * 5,
        out_specs=vmem,
        scratch_shapes=[
            pltpu.VMEM((devices, chans // 2 * per_dev, 2 * GROUP), jnp.float32),
            pltpu.VMEM((devices, 8, width), jnp.float32),
            pltpu.VMEM((2 * wide, 4 * GROUP), jnp.bfloat16),
            pltpu.VMEM((2, 4 * GROUP, width), jnp.bfloat16),
            pltpu.VMEM((2, 2, wide, width), jnp.bfloat16),
            pltpu.VMEM((wide, wide), jnp.float32),
        ]
        + [pltpu.SemaphoreType.DMA((chips,))] * 8,
        compiler_params=pltpu.CompilerParams(collective_id=0, has_side_effects=True),
    )(tile_map, channels, positions, flux, cluster[None], jones, station_uvw)


def solution(mesh):
    in_specs = (
        P(None, ("group", "src")),
        P(None, ("group", "src")),
        P(("group", "src")),
        P(None, None, None, ("group", "src")),
        P(None, ("group", "src")),
        P("group"),
        P("group", None),
    )
    out_specs = P(("group", "src"), None, None, None)
    return jax.shard_map(
        on_device, mesh=mesh, in_specs=in_specs, out_specs=out_specs, check_vma=False
    )
```

```python
import functools
import math

import jax
import jax.numpy as jnp
from jax import lax
from jax.experimental import pallas as pl
from jax.experimental.pallas import tpu as pltpu
from jax.sharding import PartitionSpec as P

MESH = pl.DeviceIdType.MESH
TS = 32
GROUP = 64
HALF = 48
CHUNK = 256
SINE = (3.1415820121765137, -5.167142868041992, 2.5418992042541504, -0.5546366572380066)
ATAN = (
    0.15915492177009583,
    -0.05305047705769539,
    0.031808558851480484,
    -0.022538291290402412,
    0.016709571704268456,
    -0.011514591053128242,
    0.006331328768283129,
    -0.0022920165210962296,
    0.00039099203422665596,
)
ONE = 1.0 + 6e-7


def horner(coefs, y):
    total = jnp.float32(coefs[-1])
    for coef in coefs[-2::-1]:
        total = total * y + jnp.float32(coef)
    return total


def three_parts(value):
    first = value.astype(jnp.bfloat16).astype(jnp.float32)
    rest = value - first
    second = rest.astype(jnp.bfloat16).astype(jnp.float32)
    return first, second, rest - second


def polar(real, imag):
    wide, tall = jnp.abs(real), jnp.abs(imag)
    large, small = jnp.maximum(wide, tall), jnp.minimum(wide, tall)
    ratio = small / jnp.where(large > 0.0, large, 1.0)
    square = ratio * ratio
    size = large * jnp.sqrt(1.0 + square)
    angle = ratio * horner(ATAN, square)
    angle = jnp.where(tall > wide, 0.25 - angle, angle)
    angle = jnp.where(real < 0.0, 0.5 - angle, angle)
    return size, jnp.where(imag < 0.0, -angle, angle)


def kernel(
    devices,
    chans,
    dirs,
    scale,
    tile_ref,
    channel_ref,
    position_ref,
    flux_ref,
    cluster_ref,
    jones_ref,
    uvw_ref,
    out_ref,
    stations,
    sources,
    table,
    onehots,
    sides,
    acc,
    st_send,
    st_recv,
    st_fwd_send,
    st_fwd_recv,
    so_send,
    so_recv,
    so_fwd_send,
    so_fwd_recv,
):
    chips = devices // 2
    me = lax.axis_index("src")
    chip = me // 2
    core = lax.rem(me, 2)
    partner = chip * 2 + 1 - core
    rows = stations.shape[1]
    per_dev = rows * 2 // chans
    width = sources.shape[2]

    barrier = pltpu.get_barrier_semaphore()

    def greet(k, carry):
        there = lax.rem(chip + k, chips) * 2 + core
        pl.semaphore_signal(barrier, inc=1, device_id={"src": there}, device_id_type=MESH)
        return carry

    pl.semaphore_signal(barrier, inc=1, device_id={"src": partner}, device_id_type=MESH)
    lax.fori_loop(1, chips, greet, 0)

    l_own, m_own = position_ref[0:1, :], position_ref[1:2, :]
    sources[me, 0:2, :] = position_ref[...]
    sources[me, 2 : 2 + chans, :] = flux_ref[...]
    sources[me, 2 + chans : 3 + chans, :] = cluster_ref[...].astype(jnp.float32)
    sources[me, 3 + chans : 4 + chans, :] = jnp.sqrt(1.0 - l_own * l_own - m_own * m_own) - 1.0
    eight = lax.broadcasted_iota(jnp.int32, (8, per_dev), 0)
    coords = jnp.where(eight == 0, uvw_ref[0:1, :], 0.0)
    coords = jnp.where(eight == 1, uvw_ref[1:2, :], coords)
    coords = jnp.where(eight == 3 + chans, uvw_ref[2:3, :], coords)
    for pair in range(chans // 2):
        features = []
        for c in (2 * pair, 2 * pair + 1):
            freq_ratio = 1.0 + 0.002 * channel_ref[c].astype(jnp.float32)
            size, angle = polar(jones_ref[c, 0], jones_ref[c, 1])
            shifted = coords * freq_ratio
            features += [-angle, shifted, shifted, shifted]
            features += [jnp.zeros((HALF - dirs - 24, per_dev), jnp.float32), 2.0 * size]
        stations[me, pair * per_dev : (pair + 1) * per_dev, :] = jnp.concatenate(features, 0).T

    pl.semaphore_wait(barrier, chips)

    def direct(mine, slots, send, recv, k):
        there = lax.rem(chip + k, chips) * 2 + core
        return pltpu.make_async_remote_copy(
            src_ref=mine,
            dst_ref=slots.at[me],
            send_sem=send.at[k],
            recv_sem=recv.at[k],
            device_id={"src": there},
            device_id_type=MESH,
        )

    def arrival(mine, slots, send, recv, k):
        came = lax.rem(chip - k + chips, chips) * 2 + core
        return pltpu.make_async_remote_copy(
            src_ref=mine,
            dst_ref=slots.at[came],
            send_sem=send.at[k],
            recv_sem=recv.at[k],
            device_id={"src": partner},
            device_id_type=MESH,
        )

    def forward(slots, send, recv, k):
        came = lax.rem(chip - k + chips, chips) * 2 + core
        return pltpu.make_async_remote_copy(
            src_ref=slots.at[came],
            dst_ref=slots.at[came],
            send_sem=send.at[k],
            recv_sem=recv.at[k],
            device_id={"src": partner},
            device_id_type=MESH,
        )

    def forwarded(slots, send, recv, k):
        came = lax.rem(chip - k + chips, chips) * 2 + 1 - core
        return pltpu.make_async_remote_copy(
            src_ref=slots.at[came],
            dst_ref=slots.at[came],
            send_sem=send.at[k],
            recv_sem=recv.at[k],
            device_id={"src": partner},
            device_id_type=MESH,
        )

    forward(stations, st_fwd_send, st_fwd_recv, 0).start()

    def send_stations(k, carry):
        direct(stations.at[me], stations, st_send, st_recv, k).start()
        return carry

    lax.fori_loop(1, chips, send_stations, 0)
    forward(sources, so_fwd_send, so_fwd_recv, 0).start()

    def send_sources(k, carry):
        direct(sources.at[me], sources, so_send, so_recv, k).start()
        return carry

    lax.fori_loop(1, chips, send_sources, 0)

    onehots[:, 3 * GROUP :, :] = jnp.zeros((2, GROUP, width), jnp.bfloat16)
    sides[1] = jnp.zeros(sides.shape[1:], jnp.bfloat16)
    acc[...] = jnp.zeros_like(acc)

    def relay_stations(k, carry):
        arrival(stations.at[me], stations, st_send, st_recv, k).wait_recv()
        forward(stations, st_fwd_send, st_fwd_recv, k).start()
        return carry

    lax.fori_loop(1, chips, relay_stations, 0)

    def take_stations(k, carry):
        forwarded(stations, st_fwd_send, st_fwd_recv, k).wait_recv()
        return carry

    lax.fori_loop(0, chips, take_stations, 0)

    per_tile = TS // per_dev
    lane = lax.broadcasted_iota(jnp.int32, (TS, 128), 1)
    is_phase = lax.rem(lane, GROUP) < HALF
    low = lane < GROUP
    half_rows = chans * TS
    tiles = [tile_ref[me, 0], tile_ref[me, 1]]
    for side in range(2):
        held = [stations[tiles[side] * per_tile + d] for d in range(per_tile)]
        for c in range(chans):
            begin = c // 2 * per_dev
            value = jnp.concatenate([part[begin : begin + per_dev] for part in held], 0)
            if c % 2:
                value = pltpu.roll(value, GROUP, 1)
            value = jnp.where(low, value, 0.0)
            first, second, third = three_parts(value)
            pieces = [first + pltpu.roll(second, GROUP, 1), third]
            at = (side * chans + c) * 2 * TS
            for index, piece in enumerate(pieces):
                cols = slice(index * 128, index * 128 + 128)
                table[at : at + TS, cols] = jnp.where(is_phase, piece, 0.0).astype(jnp.bfloat16)
                below = at + TS
                table[below : below + TS, cols] = jnp.where(is_phase, 0.0, piece).astype(
                    jnp.bfloat16
                )

    contract = (((1,), (1,)), ((), ()))

    def predict(slot, came):
        rows_in = sources[came]
        kinds = rows_in[2 + chans : 3 + chans, :]
        parts = three_parts(rows_in) + (jnp.zeros_like(rows_in),)
        kind_rows = lax.broadcasted_iota(jnp.int32, (dirs, width), 0).astype(jnp.float32)
        onehot = jnp.where(kind_rows == kinds, 1.0, 0.0).astype(jnp.bfloat16)
        upper = jnp.concatenate(parts[:2], 0).astype(jnp.bfloat16)
        lower = jnp.concatenate(parts[2:], 0).astype(jnp.bfloat16)
        for part in range(3):
            base = part * GROUP
            for index, value in enumerate((onehot, upper, lower, onehot)):
                onehots[slot, base + index * 16 : base + index * 16 + 16, :] = value

        for chunk in range(width // CHUNK):
            cols = slice(chunk * CHUNK, chunk * CHUNK + CHUNK)
            weights = onehots[slot, :, cols]
            found = jnp.dot(table[...], weights, preferred_element_type=jnp.float32)
            for side in range(2):
                for c in range(chans):
                    at = (side * chans + c) * 2 * TS
                    turns = found[at : at + TS]
                    double = found[at + TS : at + 2 * TS]
                    if side == 0:
                        double = double * (sources[came, 2 + c : 3 + c, cols] * scale)
                    turns = turns - jnp.round(turns)
                    sine = turns * horner(SINE, turns * turns)
                    square = sine * sine
                    rest = ONE - square
                    cosine = rest * lax.rsqrt(rest)
                    real = double * (0.5 - square)
                    imag = (double * sine) * cosine
                    top = c * TS
                    sides[slot, side, top : top + TS, cols] = real.astype(jnp.bfloat16)
                    sides[slot, side, half_rows + top : half_rows + top + TS, cols] = imag.astype(
                        jnp.bfloat16
                    )

    def add_products(slot):
        acc[...] += lax.dot_general(
            sides[slot, 0], sides[slot, 1], contract, preferred_element_type=jnp.float32
        )

    def step(k, carry):
        came = lax.rem(chip - k + chips, chips) * 2
        predict(0, came + core)
        add_products(1)

        @pl.when(k + 1 < chips)
        def _():
            arrival(sources.at[me], sources, so_send, so_recv, k + 1).wait_recv()
            forward(sources, so_fwd_send, so_fwd_recv, k + 1).start()

        forwarded(sources, so_fwd_send, so_fwd_recv, k).wait_recv()
        predict(1, came + 1 - core)
        add_products(0)
        return carry

    lax.fori_loop(0, chips, step, 0)
    add_products(1)

    same = tiles[0] == tiles[1]
    diagonal = lax.broadcasted_iota(jnp.int32, (TS, TS), 0) == lax.broadcasted_iota(
        jnp.int32, (TS, TS), 1
    )
    clear = jnp.logical_and(diagonal, same)
    for c in range(chans):
        top = slice(c * TS, c * TS + TS)
        low_rows = slice(half_rows + c * TS, half_rows + c * TS + TS)
        real_rows = acc[top, :]
        imag_rows = acc[low_rows, :]
        real = real_rows[:, top] + imag_rows[:, low_rows]
        imag = real_rows[:, low_rows] - imag_rows[:, top]
        for part, value in enumerate((real, imag)):
            value = jnp.where(clear, 0.0, value)
            for i in range(TS):
                out_ref[0, c, part : part + 1, i * TS : i * TS + TS] = value[i : i + 1, :]

    def finish(k, carry):
        direct(stations.at[me], stations, st_send, st_recv, k).wait_send()
        direct(sources.at[me], sources, so_send, so_recv, k).wait_send()
        return carry

    lax.fori_loop(1, chips, finish, 0)

    def finish_forward(k, carry):
        forward(stations, st_fwd_send, st_fwd_recv, k).wait_send()
        forward(sources, so_fwd_send, so_fwd_recv, k).wait_send()
        return carry

    lax.fori_loop(0, chips, finish_forward, 0)


def on_device(positions, flux, cluster, jones, station_uvw, channels, tile_map):
    width = positions.shape[1]
    devices = lax.axis_size("src")
    scale = 1.0 / math.sqrt(width * devices)
    chans, _, dirs, per_dev = jones.shape

    wide = 2 * chans * TS
    chips = devices // 2
    vmem = pl.BlockSpec(memory_space=pltpu.VMEM)
    return pl.pallas_call(
        functools.partial(kernel, devices, chans, dirs, scale),
        out_shape=jax.ShapeDtypeStruct((1, chans, 2, TS * TS), jnp.float32),
        in_specs=[pl.BlockSpec(memory_space=pltpu.SMEM)] * 2 + [vmem] * 5,
        out_specs=vmem,
        scratch_shapes=[
            pltpu.VMEM((devices, chans // 2 * per_dev, 2 * GROUP), jnp.float32),
            pltpu.VMEM((devices, 8, width), jnp.float32),
            pltpu.VMEM((2 * wide, 4 * GROUP), jnp.bfloat16),
            pltpu.VMEM((2, 4 * GROUP, width), jnp.bfloat16),
            pltpu.VMEM((2, 2, wide, width), jnp.bfloat16),
            pltpu.VMEM((wide, wide), jnp.float32),
        ]
        + [pltpu.SemaphoreType.DMA((chips,))] * 8,
        compiler_params=pltpu.CompilerParams(collective_id=0, has_side_effects=True),
    )(tile_map, channels, positions, flux, cluster[None], jones, station_uvw)


def solution(mesh):
    in_specs = (
        P(None, ("group", "src")),
        P(None, ("group", "src")),
        P(("group", "src")),
        P(None, None, None, ("group", "src")),
        P(None, ("group", "src")),
        P("group"),
        P("group", None),
    )
    out_specs = P(("group", "src"), None, None, None)
    return jax.shard_map(
        on_device, mesh=mesh, in_specs=in_specs, out_specs=out_specs, check_vma=False
    )
```
